32 devices in a mesh: cuts: 1, state: 32 (over z, y, x, core).
Axes of the slice: x: 2, y: 2, z: 4, core: 2. Of those that a mesh axis runs over, the one named last changes fastest.
Arguments:
- initial_states: bfloat16 [256, 32, 48, 128], P(('cuts', 'state')), may hold values from -36 to 36
- potential: float32 [32, 48, 128], replicated, may hold values from -1 to 0
- bounds: int32 [2], P('cuts'), may hold values from -32 to 159, as said below
Outputs:
- orthonormal: float32 [256, 196608], P('cuts', 'state')
The draws below stay inside these ranges and needn't reach their ends.
Inputs may be any that keep to these rules, and one draw needn't show every extreme that they name: `bounds`: the first entry lies in -32 to -17, inside the spectrum of H, and the second in 136 to 159, above it; the anchor -1.125 lies below the spectrum.
All inputs are finite; a program needn't handle non-finite values.
Results may differ from the reference program's by a relative error of at most 0.0003.
Values sent between devices are 32-bit elements; how exact they have to be, the bound alone decides.
No kernel may reach another device: no remote copies, remote signals or barrier semaphores. Data moves between devices by JAX's collectives and lax.ppermute only.
A program may use at most 192 MiB of HBM per device.

```python
import math
import jax
import jax.numpy as jnp
from jax import lax

NST = 256
GZ = 32
GX = 48
GY = 128
DEGREE = 16


def draw_initial_states(key, part):
    key_rows, key_cols, key_base = jax.random.split(jax.random.fold_in(key, 11), 3)
    points = GZ * GX * GY
    log_span = math.log(10.0)
    row_scale = 0.3 * jnp.exp(jax.random.uniform(key_rows, (points,), jnp.float32, 0.0, log_span))
    col_scale = 0.3 * jnp.exp(jax.random.uniform(key_cols, (NST,), jnp.float32, 0.0, log_span))
    base_draw = jnp.clip(jax.random.normal(key_base, (NST, points), jnp.float32), -4.0, 4.0)
    values = base_draw * row_scale[None, :] * col_scale[:, None]
    return values.reshape(NST, GZ, GX, GY).astype(jnp.bfloat16)


def draw_bounds(key, part):
    key_low, key_high = jax.random.split(jax.random.fold_in(key, 23))
    low_end = jax.random.randint(key_low, (1,), -32, -16)
    high_end = jax.random.randint(key_high, (1,), 136, 160)
    return jnp.concatenate([low_end, high_end]).astype(jnp.int32)


def setup_inputs(seed: int = 0, part: int = 0) -> dict:
    streams_of = jax.random.split(jax.random.key(seed), 4)
    part_splits = jax.random.split(jax.random.fold_in(streams_of[3], part), 4)
    initial_states = draw_initial_states(jax.random.fold_in(jax.random.fold_in(streams_of[3], part), 71), part)
    potential = jnp.clip(jax.random.uniform(streams_of[1], (GZ, GX, GY), jnp.float32, -1.0, 0.0), -1.0, 0.0)
    bounds = draw_bounds(jax.random.fold_in(jax.random.fold_in(streams_of[3], part), 71), part)
    return {"initial_states": initial_states, "potential": potential, "bounds": bounds}


STENCIL_NEAR = 4.0 / 3.0
STENCIL_FAR = -1.0 / 12.0
STENCIL_SELF = -5.0 / 2.0
ANCHOR_VALUE = -1.125

def laplace_periodic(values, axis_dim):
    near_sum = jnp.roll(values, 1, axis_dim) + jnp.roll(values, -1, axis_dim)
    far_sum = jnp.roll(values, 2, axis_dim) + jnp.roll(values, -2, axis_dim)
    return STENCIL_NEAR * near_sum + STENCIL_FAR * far_sum

def laplace_walled(values):
    extent = values.shape[1]
    padded = jnp.pad(values, ((0, 0), (2, 2), (0, 0), (0, 0)))
    near_sum = padded[:, 1:extent + 1] + padded[:, 3:extent + 3]
    far_sum = padded[:, 0:extent] + padded[:, 4:extent + 4]
    return STENCIL_NEAR * near_sum + STENCIL_FAR * far_sum

def apply_hamiltonian(values, potential):
    laplace = 3.0 * STENCIL_SELF * values + laplace_walled(values)
    laplace = laplace + laplace_periodic(values, 2) + laplace_periodic(values, 3)
    return -0.5 * laplace + potential[None] * values

def filter_states(states, potential, bounds):
    low_end = bounds[0].astype(jnp.float32) / 64.0
    high_end = bounds[1].astype(jnp.float32) / 16.0
    half_width = (high_end - low_end) / 2.0
    centre = (high_end + low_end) / 2.0
    sigma_now = half_width / (ANCHOR_VALUE - centre)
    tau_value = 2.0 / sigma_now
    current = (apply_hamiltonian(states, potential) - centre * states) * (sigma_now / half_width)

    def degree_step(degree, carried):
        previous, current, sigma_now = carried
        sigma_next = 1.0 / (tau_value - sigma_now)
        latest = (apply_hamiltonian(current, potential) - centre * current) * (2.0 * sigma_next / half_width)
        latest = latest - sigma_now * sigma_next * previous
        return (current, latest, sigma_next)
    carried = lax.fori_loop(1, DEGREE, degree_step, (states, current, sigma_now))
    return carried[1]

def reference(initial_states, potential, bounds):
    filtered = filter_states(initial_states.astype(jnp.float32), potential, bounds)
    flat = filtered.reshape(NST, GZ * GX * GY)
    gram = lax.dot_general(flat.astype(jnp.float32), flat.astype(jnp.float32), (((1,), (1,)), ((), ())), precision=lax.Precision.HIGHEST, preferred_element_type=jnp.float32)
    factor = jnp.linalg.cholesky(gram)
    solved = lax.linalg.triangular_solve(factor, flat, left_side=True, lower=True)
    return solved * math.sqrt(GZ * GX * GY)
```

```python
import functools
import math

import jax
import jax.numpy as jnp
from jax import lax
from jax.experimental import pallas as pl
from jax.experimental.pallas import tpu as pltpu
from jax.sharding import PartitionSpec as P

DEGREE = 16
ANCHOR_VALUE = -1.125
SUB = 8
LANES = 128
BLOCK = 32
VMEM_LIMIT = 60 * 2**20


def filter_scalars(bounds):
    low_end = bounds[0].astype(jnp.float32) / 64.0
    high_end = bounds[1].astype(jnp.float32) / 16.0
    half_width = (high_end - low_end) / 2.0
    centre = (high_end + low_end) / 2.0
    sigma_now = half_width / (ANCHOR_VALUE - centre)
    tau_value = 2.0 / sigma_now
    scale = sigma_now
    for _ in range(1, DEGREE):
        sigma_now = 1.0 / (tau_value - sigma_now)
        scale = scale * sigma_now
    return jnp.stack(
        [
            (-1.0 / 12.0) / half_width,
            2.0 / half_width,
            3.75 - centre,
            scale,
        ]
    )


def filter_kernel(scal, states, potential, out, weight, first, second):
    depth, rows, lanes = out.shape
    tiles = rows // SUB
    planes = depth
    line_w, twice, shift, scale = (scal[i] for i in range(4))

    @pl.when(pl.program_id(0) == 0)
    def _():
        @pl.loop(0, depth, unroll=8)
        def _(z):
            for t in range(tiles):
                piece = potential[z, pl.ds(t, SUB, stride=tiles), :]
                weight[z, t] = (piece + shift) * twice

        for field in (first, second):
            for edge in (0, 1, depth + 2, depth + 3):
                field[edge] = jnp.zeros(field.shape[1:], jnp.float32)

    @pl.loop(0, depth, unroll=8)
    def _(z):
        out[z] = states[z].astype(jnp.float32)
        for t in range(tiles):
            first[z + 2, t] = out[z, pl.ds(t, SUB, stride=tiles), :]

    wrap = lax.broadcasted_iota(jnp.int32, (lanes, lanes), 0)
    wrap = jnp.abs(wrap - lax.broadcasted_iota(jnp.int32, (lanes, lanes), 1))
    wrap = jnp.minimum(wrap, lanes - wrap)
    ring = jnp.where(wrap == 1, 16.0, jnp.where(wrap == 2, -1.0, 0.0)).astype(jnp.bfloat16)
    ring = jnp.concatenate([ring, ring], axis=0)

    def applied(src, base):
        block = src[pl.ds(base + 2, planes)]
        along = block.reshape(planes * rows, lanes)
        along = dot(jnp.concatenate(split(along), axis=1), ring, ((1,), (0,)))
        along = along.reshape(block.shape)
        for p in range(planes):
            z = base + p
            held = [block[p, t] for t in range(tiles)]
            back = {t: pltpu.roll(held[t], 1, 0) for t in (tiles - 1, tiles - 2)}
            ahead = {t: pltpu.roll(held[t], SUB - 1, 0) for t in (0, 1)}

            def at(t):
                if t < 0:
                    return back[t + tiles]
                if t >= tiles:
                    return ahead[t - tiles]
                return held[t]

            for t in range(tiles):
                near = (at(t - 1) + at(t + 1)) + (src[z + 1, t] + src[z + 3, t])
                far = (at(t - 2) + at(t + 2)) + (src[z, t] + src[z + 4, t])
                total = along[p, t] + (16.0 * near - far)
                yield z, t, total * line_w + held[t] * weight[z, t]

    def step(src, dst):
        @pl.loop(0, depth // planes)
        def _(i):
            for z, t, value in applied(src, i * planes):
                dst[z + 2, t] = value - dst[z + 2, t]

    @pl.loop(0, depth // planes)
    def _(i):
        for z, t, value in applied(first, i * planes):
            second[z + 2, t] = 0.5 * value

    @pl.loop(0, (DEGREE - 2) // 2)
    def _(_):
        step(second, first)
        step(first, second)

    @pl.loop(0, depth // planes)
    def _(i):
        for z, t, value in applied(second, i * planes):
            final = (value - first[z + 2, t]) * scale
            out[z, pl.ds(t, SUB, stride=tiles), :] = final


def run_filter(scal, states, potential, begin, count):
    _, depth, rows, lanes = states.shape
    field = pltpu.VMEM((depth + 4, rows // SUB, SUB, lanes), jnp.float32)
    points = depth * rows * lanes
    return pl.pallas_call(
        filter_kernel,
        grid=(count,),
        in_specs=[
            pl.BlockSpec(memory_space=pltpu.SMEM),
            pl.BlockSpec((None, depth, rows, lanes), lambda i: (begin + i, 0, 0, 0)),
            pl.BlockSpec((depth, rows, lanes), lambda i: (0, 0, 0)),
        ],
        out_specs=pl.BlockSpec((depth, None, rows, lanes), lambda i: (0, i, 0, 0)),
        out_shape=jax.ShapeDtypeStruct((depth, count, rows, lanes), jnp.float32),
        scratch_shapes=[
            pltpu.VMEM((depth, rows // SUB, SUB, lanes), jnp.float32),
            field,
            field,
        ],
        compiler_params=pltpu.CompilerParams(dimension_semantics=("arbitrary",)),
        cost_estimate=pl.CostEstimate(
            flops=18 * DEGREE * points * count,
            bytes_accessed=points * (6 * count + 4),
            transcendentals=0,
        ),
        name=f"filter_{begin}",
    )(scal, states, potential)


def split(value):
    high = value.astype(jnp.bfloat16)
    return high, (value - high.astype(jnp.float32)).astype(jnp.bfloat16)


def dot(left, right, dims):
    return lax.dot_general(left, right, (dims, ((), ())), preferred_element_type=jnp.float32)


def gram_kernel(counts, aligned, *refs):
    pieces, flat, gram, gram_high, gram_cross = refs[:-4], *refs[-4:]
    i = pl.program_id(0)
    first_state = 0
    per_device = sum(counts)
    for piece, count in zip(pieces, counts):
        if aligned:
            sources, _, rows, lanes = piece.shape
            lines = piece.reshape(sources * count * rows, lanes)
        else:
            _, rows, sources, lanes = piece.shape
        for j in range(count):
            for r in range(rows):
                if aligned:
                    value = lines[pl.ds(j * rows + r, sources, stride=count * rows), :]
                else:
                    value = piece[j, r]
                flat[r, pl.ds(first_state + j, sources, stride=per_device), :] = value
        first_state += count
    high, low = split(jnp.concatenate([flat[r] for r in range(flat.shape[0])], axis=1))
    now_high = dot(high, high, ((1,), (1,)))
    now_cross = dot(high, low, ((1,), (1,)))

    @pl.when(i == 0)
    def _():
        gram_high[...] = now_high
        gram_cross[...] = now_cross

    @pl.when(i > 0)
    def _():
        gram_high[...] += now_high
        gram_cross[...] += now_cross

    @pl.when(i == pl.num_programs(0) - 1)
    def _():
        cross = gram_cross[...]
        gram[...] = gram_high[...] + (cross + cross.T)


def run_gram(pieces):
    counts = tuple(p.shape[1] for p in pieces)
    sources, _, rows, lanes = pieces[0].shape
    states = sources * sum(counts)
    tall = SUB if rows % SUB == 0 else rows
    specs = [pl.BlockSpec((sources, c, tall, lanes), lambda i: (0, 0, i, 0)) for c in counts]
    if rows % SUB:
        pieces = [jnp.transpose(p, (1, 2, 0, 3)) for p in pieces]
        specs = [pl.BlockSpec(p.shape, lambda i: (0, 0, 0, 0)) for p in pieces]
    return pl.pallas_call(
        functools.partial(gram_kernel, counts, rows % SUB == 0),
        grid=(rows // tall,),
        in_specs=specs,
        out_specs=[
            pl.BlockSpec((tall, states, lanes), lambda i: (i, 0, 0)),
            pl.BlockSpec((states, states), lambda i: (0, 0)),
        ],
        out_shape=[
            jax.ShapeDtypeStruct((rows, states, lanes), jnp.float32),
            jax.ShapeDtypeStruct((states, states), jnp.float32),
        ],
        scratch_shapes=[pltpu.VMEM((states, states), jnp.float32)] * 2,
        compiler_params=pltpu.CompilerParams(dimension_semantics=("arbitrary",)),
        name="gram",
    )(*pieces)


def exact_dot(left, right, dims):
    return lax.dot_general(
        left,
        right,
        (dims, ((), ())),
        precision=lax.Precision.HIGHEST,
        preferred_element_type=jnp.float32,
    )


def factor_kernel(factor_scale, gram, high, low, work):
    size = gram.shape[0]
    work[:, :size] = gram[...]
    rows = lax.broadcasted_iota(jnp.int32, (size, size), 0)
    cols = lax.broadcasted_iota(jnp.int32, (size, size), 1)
    work[:, size:] = jnp.where(rows == cols, 1.0, 0.0)
    lane = lax.broadcasted_iota(jnp.int32, (BLOCK, LANES), 1)
    line = lax.broadcasted_iota(jnp.int32, (BLOCK, LANES), 0)
    for k in range(0, size, BLOCK):
        diag = work[k : k + BLOCK, k : k + BLOCK]
        unit = jnp.where(lane == line + BLOCK, 1.0, 0.0)
        local = jnp.concatenate([diag, unit[:, BLOCK:]], axis=1)
        pivots = jnp.ones((BLOCK, LANES), jnp.float32)
        for j in range(BLOCK):
            column = jnp.broadcast_to(local[:, j : j + 1], (BLOCK, LANES))
            pivot = column[j : j + 1, :]
            ratio = jnp.where(line > j, column / pivot, 0.0)
            pivots = jnp.where(line == j, jnp.broadcast_to(pivot, pivots.shape), pivots)
            local = local - ratio * local[j : j + 1, :]
        inverse = (local * lax.rsqrt(pivots))[:, BLOCK : 2 * BLOCK]
        panel = exact_dot(inverse, work[k : k + BLOCK, :], ((1,), (0,)))
        work[k : k + BLOCK, :] = panel
        if k + BLOCK < size:
            below = panel[:, k + BLOCK : size]
            work[k + BLOCK :, :] -= exact_dot(below, panel, ((0,), (0,)))
    result = work[:, size:] * factor_scale
    high[...], low[...] = split(result)


def run_factor(gram, factor_scale):
    shape = jax.ShapeDtypeStruct(gram.shape, jnp.bfloat16)
    size = gram.shape[0]
    return pl.pallas_call(
        functools.partial(factor_kernel, factor_scale),
        out_shape=[shape, shape],
        scratch_shapes=[pltpu.VMEM((size, 2 * size), jnp.float32)],
        name="factor",
    )(gram)


def apply_kernel(high, low, flat, out):
    flat_high, flat_low = split(jnp.concatenate([flat[r] for r in range(flat.shape[0])], axis=1))
    total = dot(high[...], flat_low, ((1,), (0,))) + dot(low[...], flat_high, ((1,), (0,)))
    out[...] = dot(high[...], flat_high, ((1,), (0,))) + total


def run_apply(high, low, flat):
    rows, states, lanes = flat.shape
    tall = SUB if rows % SUB == 0 else rows
    whole = pl.BlockSpec((states, states), lambda i: (0, 0))
    return pl.pallas_call(
        apply_kernel,
        grid=(rows // tall,),
        in_specs=[whole, whole, pl.BlockSpec((tall, states, lanes), lambda i: (i, 0, 0))],
        out_specs=pl.BlockSpec((states, tall * lanes), lambda i: (0, i)),
        out_shape=jax.ShapeDtypeStruct((states, rows * lanes), jnp.float32),
        compiler_params=pltpu.CompilerParams(dimension_semantics=("arbitrary",)),
        name="apply",
    )(high, low, flat)


def chunk_counts(states):
    rest = states - 1
    return [c for c in (1, rest // 2, rest - rest // 2) if c]


def per_device(devices, initial_states, potential, bounds):
    states, depth, rows, lanes = initial_states.shape
    points = depth * rows * lanes
    local = points // devices
    scal = filter_scalars(bounds)
    pieces = []
    begin = 0
    for count in chunk_counts(states):
        filtered = run_filter(scal, initial_states, potential, begin, count)
        if devices != depth:
            filtered = jnp.swapaxes(filtered, 0, 1).reshape(count, devices, local // lanes, lanes)
            filtered = jnp.swapaxes(filtered, 0, 1)
        pieces.append(lax.all_to_all(filtered, "state", split_axis=0, concat_axis=0, tiled=True))
        begin += count
    flat, gram = run_gram(pieces)
    total = gram.shape[0]
    blocks = gram.reshape(devices, total // devices, total)
    blocks = lax.all_to_all(blocks, "state", split_axis=0, concat_axis=0, tiled=True)
    mine = jnp.broadcast_to(jnp.sum(blocks, axis=0)[None], blocks.shape)
    gram = lax.all_to_all(mine, "state", split_axis=0, concat_axis=0, tiled=True)
    high, low = run_factor(gram.reshape(total, total), math.sqrt(points))
    return run_apply(high, low, flat)


def solution(mesh):
    return jax.shard_map(
        functools.partial(per_device, mesh.shape["state"]),
        mesh=mesh,
        in_specs=(P(("cuts", "state"), None, None, None), P(), P("cuts")),
        out_specs=P("cuts", "state"),
        check_vma=False,
    )
```

```python
import functools
import math

import jax
import jax.numpy as jnp
from jax import lax
from jax.experimental import pallas as pl
from jax.experimental.pallas import tpu as pltpu
from jax.sharding import PartitionSpec as P

DEGREE = 16
ANCHOR_VALUE = -1.125
SUB = 8
LANES = 128
BLOCK = 32
VMEM_LIMIT = 60 * 2**20


def filter_scalars(bounds):
    low_end = bounds[0].astype(jnp.float32) / 64.0
    high_end = bounds[1].astype(jnp.float32) / 16.0
    half_width = (high_end - low_end) / 2.0
    centre = (high_end + low_end) / 2.0
    sigma_now = half_width / (ANCHOR_VALUE - centre)
    tau_value = 2.0 / sigma_now
    scale = sigma_now
    for _ in range(1, DEGREE):
        sigma_now = 1.0 / (tau_value - sigma_now)
        scale = scale * sigma_now
    return jnp.stack(
        [
            (-1.0 / 12.0) / half_width,
            2.0 / half_width,
            3.75 - centre,
            scale,
        ]
    )


def filter_kernel(scal, states, potential, out, weight, first, second):
    depth, rows, lanes = out.shape
    tiles = rows // SUB
    planes = depth
    line_w, twice, shift, scale = (scal[i] for i in range(4))

    @pl.when(pl.program_id(0) == 0)
    def _():
        @pl.loop(0, depth, unroll=8)
        def _(z):
            for t in range(tiles):
                piece = potential[z, pl.ds(t, SUB, stride=tiles), :]
                weight[z, t] = (piece + shift) * twice

        for field in (first, second):
            for edge in (0, 1, depth + 2, depth + 3):
                field[edge] = jnp.zeros(field.shape[1:], jnp.float32)

    @pl.loop(0, depth, unroll=8)
    def _(z):
        out[z] = states[z].astype(jnp.float32)
        for t in range(tiles):
            first[z + 2, t] = out[z, pl.ds(t, SUB, stride=tiles), :]

    wrap = lax.broadcasted_iota(jnp.int32, (lanes, lanes), 0)
    wrap = jnp.abs(wrap - lax.broadcasted_iota(jnp.int32, (lanes, lanes), 1))
    wrap = jnp.minimum(wrap, lanes - wrap)
    ring = jnp.where(wrap == 1, 16.0, jnp.where(wrap == 2, -1.0, 0.0)).astype(jnp.bfloat16)
    ring = jnp.concatenate([ring, ring], axis=0)

    def applied(src, base):
        block = src[pl.ds(base + 2, planes)]
        along = block.reshape(planes * rows, lanes)
        along = dot(jnp.concatenate(split(along), axis=1), ring, ((1,), (0,)))
        along = along.reshape(block.shape)
        for p in range(planes):
            z = base + p
            held = [block[p, t] for t in range(tiles)]
            back = {t: pltpu.roll(held[t], 1, 0) for t in (tiles - 1, tiles - 2)}
            ahead = {t: pltpu.roll(held[t], SUB - 1, 0) for t in (0, 1)}

            def at(t):
                if t < 0:
                    return back[t + tiles]
                if t >= tiles:
                    return ahead[t - tiles]
                return held[t]

            for t in range(tiles):
                near = (at(t - 1) + at(t + 1)) + (src[z + 1, t] + src[z + 3, t])
                far = (at(t - 2) + at(t + 2)) + (src[z, t] + src[z + 4, t])
                total = along[p, t] + (16.0 * near - far)
                yield z, t, total * line_w + held[t] * weight[z, t]

    def step(src, dst):
        @pl.loop(0, depth // planes)
        def _(i):
            for z, t, value in applied(src, i * planes):
                dst[z + 2, t] = value - dst[z + 2, t]

    @pl.loop(0, depth // planes)
    def _(i):
        for z, t, value in applied(first, i * planes):
            second[z + 2, t] = 0.5 * value

    @pl.loop(0, (DEGREE - 2) // 2)
    def _(_):
        step(second, first)
        step(first, second)

    @pl.loop(0, depth // planes)
    def _(i):
        for z, t, value in applied(second, i * planes):
            final = (value - first[z + 2, t]) * scale
            out[z, pl.ds(t, SUB, stride=tiles), :] = final


def run_filter(scal, states, potential, begin, count):
    _, depth, rows, lanes = states.shape
    field = pltpu.VMEM((depth + 4, rows // SUB, SUB, lanes), jnp.float32)
    points = depth * rows * lanes
    return pl.pallas_call(
        filter_kernel,
        grid=(count,),
        in_specs=[
            pl.BlockSpec(memory_space=pltpu.SMEM),
            pl.BlockSpec((None, depth, rows, lanes), lambda i: (begin + i, 0, 0, 0)),
            pl.BlockSpec((depth, rows, lanes), lambda i: (0, 0, 0)),
        ],
        out_specs=pl.BlockSpec((depth, None, rows, lanes), lambda i: (0, i, 0, 0)),
        out_shape=jax.ShapeDtypeStruct((depth, count, rows, lanes), jnp.float32),
        scratch_shapes=[
            pltpu.VMEM((depth, rows // SUB, SUB, lanes), jnp.float32),
            field,
            field,
        ],
        compiler_params=pltpu.CompilerParams(dimension_semantics=("arbitrary",)),
        cost_estimate=pl.CostEstimate(
            flops=18 * DEGREE * points * count,
            bytes_accessed=points * (6 * count + 4),
            transcendentals=0,
        ),
        name=f"filter_{begin}",
    )(scal, states, potential)


def split(value):
    high = value.astype(jnp.bfloat16)
    return high, (value - high.astype(jnp.float32)).astype(jnp.bfloat16)


def dot(left, right, dims):
    return lax.dot_general(left, right, (dims, ((), ())), preferred_element_type=jnp.float32)


def gram_kernel(counts, aligned, *refs):
    pieces, flat, gram, gram_high, gram_cross = refs[:-4], *refs[-4:]
    i = pl.program_id(0)
    first_state = 0
    per_device = sum(counts)
    for piece, count in zip(pieces, counts):
        if aligned:
            sources, _, rows, lanes = piece.shape
            lines = piece.reshape(sources * count * rows, lanes)
        else:
            _, rows, sources, lanes = piece.shape
        for j in range(count):
            for r in range(rows):
                if aligned:
                    value = lines[pl.ds(j * rows + r, sources, stride=count * rows), :]
                else:
                    value = piece[j, r]
                flat[r, pl.ds(first_state + j, sources, stride=per_device), :] = value
        first_state += count
    high, low = split(jnp.concatenate([flat[r] for r in range(flat.shape[0])], axis=1))
    now_high = dot(high, high, ((1,), (1,)))
    now_cross = dot(high, low, ((1,), (1,)))

    @pl.when(i == 0)
    def _():
        gram_high[...] = now_high
        gram_cross[...] = now_cross

    @pl.when(i > 0)
    def _():
        gram_high[...] += now_high
        gram_cross[...] += now_cross

    @pl.when(i == pl.num_programs(0) - 1)
    def _():
        cross = gram_cross[...]
        gram[...] = gram_high[...] + (cross + cross.T)


def run_gram(pieces):
    counts = tuple(p.shape[1] for p in pieces)
    sources, _, rows, lanes = pieces[0].shape
    states = sources * sum(counts)
    tall = SUB if rows % SUB == 0 else rows
    specs = [pl.BlockSpec((sources, c, tall, lanes), lambda i: (0, 0, i, 0)) for c in counts]
    if rows % SUB:
        pieces = [jnp.transpose(p, (1, 2, 0, 3)) for p in pieces]
        specs = [pl.BlockSpec(p.shape, lambda i: (0, 0, 0, 0)) for p in pieces]
    return pl.pallas_call(
        functools.partial(gram_kernel, counts, rows % SUB == 0),
        grid=(rows // tall,),
        in_specs=specs,
        out_specs=[
            pl.BlockSpec((tall, states, lanes), lambda i: (i, 0, 0)),
            pl.BlockSpec((states, states), lambda i: (0, 0)),
        ],
        out_shape=[
            jax.ShapeDtypeStruct((rows, states, lanes), jnp.float32),
            jax.ShapeDtypeStruct((states, states), jnp.float32),
        ],
        scratch_shapes=[pltpu.VMEM((states, states), jnp.float32)] * 2,
        compiler_params=pltpu.CompilerParams(dimension_semantics=("arbitrary",)),
        name="gram",
    )(*pieces)


def exact_dot(left, right, dims):
    return lax.dot_general(
        left,
        right,
        (dims, ((), ())),
        precision=lax.Precision.HIGHEST,
        preferred_element_type=jnp.float32,
    )


def eliminate(tiles):
    count = len(tiles)
    shape = tiles[0].shape
    line = lax.broadcasted_iota(jnp.int32, shape, 0)

    def row(tile, c):
        return jnp.broadcast_to(tile[c : c + 1, :], shape)

    cols = [
        {g: jnp.broadcast_to(tiles[g][:, d : d + 1], shape) for g in range(d // SUB, count)}
        for d in range(count * SUB)
    ]
    scales = [jnp.ones(shape, jnp.float32) for _ in range(count)]
    for j in range(0, count * SUB, 2):
        own, c = j // SUB, j % SUB
        left, right = cols[j], cols[j + 1]
        p, q, s = row(left[own], c), row(left[own], c + 1), row(right[own], c + 1)
        inverse = 1.0 / (p * s - q * q)
        p_in, q_in, s_in = p * inverse, q * inverse, s * inverse
        ratio = q / p
        row_left, row_right = row(tiles[own], c), row(tiles[own], c + 1)
        scales[own] = jnp.where(line == c, p, scales[own])
        scales[own] = jnp.where(line == c + 1, s - q * ratio, scales[own])
        first, second = {}, {}
        for g in range(own, count):
            first[g] = left[g] * s_in - right[g] * q_in
            second[g] = right[g] * p_in - left[g] * q_in
        first[own] = jnp.where(line > c + 1, first[own], jnp.where(line == c + 1, ratio, 0.0))
        second[own] = jnp.where(line > c + 1, second[own], 0.0)
        for d in range(j + 2, count * SUB):
            x, y = row(left[d // SUB], d % SUB), row(right[d // SUB], d % SUB)
            for g in range(d // SUB, count):
                cols[d][g] = cols[d][g] - (first[g] * x + second[g] * y)
        for g in range(own, count):
            tiles[g] = tiles[g] - (first[g] * row_left + second[g] * row_right)
    return [t * lax.rsqrt(v) for t, v in zip(tiles, scales)]


def factor_kernel(factor_scale, gram, high, low, work):
    size = gram.shape[0]
    work[:, :size] = gram[...]
    rows = lax.broadcasted_iota(jnp.int32, (size, size), 0)
    cols = lax.broadcasted_iota(jnp.int32, (size, size), 1)
    work[:, size:] = jnp.where(rows == cols, 1.0, 0.0)
    lane = lax.broadcasted_iota(jnp.int32, (BLOCK, LANES), 1)
    line = lax.broadcasted_iota(jnp.int32, (BLOCK, LANES), 0)
    unit = jnp.where(lane == line + BLOCK, 1.0, 0.0)
    for k in range(0, size, BLOCK):
        diag = work[k : k + BLOCK, k : k + BLOCK]
        local = jnp.concatenate([diag, unit[:, BLOCK:]], axis=1)
        tiles = eliminate([local[i : i + SUB] for i in range(0, BLOCK, SUB)])
        inverse = jnp.concatenate(tiles, axis=0)[:, BLOCK : 2 * BLOCK]
        panel = exact_dot(inverse, work[k : k + BLOCK, :], ((1,), (0,)))
        work[k : k + BLOCK, :] = panel
        if k + BLOCK < size:
            below = panel[:, k + BLOCK : size]
            work[k + BLOCK :, :] -= exact_dot(below, panel, ((0,), (0,)))
    result = work[:, size:] * factor_scale
    high[...], low[...] = split(result)


def run_factor(gram, factor_scale):
    shape = jax.ShapeDtypeStruct(gram.shape, jnp.bfloat16)
    size = gram.shape[0]
    return pl.pallas_call(
        functools.partial(factor_kernel, factor_scale),
        out_shape=[shape, shape],
        scratch_shapes=[pltpu.VMEM((size, 2 * size), jnp.float32)],
        name="factor",
    )(gram)


def apply_kernel(high, low, flat, out):
    flat_high, flat_low = split(jnp.concatenate([flat[r] for r in range(flat.shape[0])], axis=1))
    total = dot(high[...], flat_low, ((1,), (0,))) + dot(low[...], flat_high, ((1,), (0,)))
    out[...] = dot(high[...], flat_high, ((1,), (0,))) + total


def run_apply(high, low, flat):
    rows, states, lanes = flat.shape
    tall = SUB if rows % SUB == 0 else rows
    whole = pl.BlockSpec((states, states), lambda i: (0, 0))
    return pl.pallas_call(
        apply_kernel,
        grid=(rows // tall,),
        in_specs=[whole, whole, pl.BlockSpec((tall, states, lanes), lambda i: (i, 0, 0))],
        out_specs=pl.BlockSpec((states, tall * lanes), lambda i: (0, i)),
        out_shape=jax.ShapeDtypeStruct((states, rows * lanes), jnp.float32),
        compiler_params=pltpu.CompilerParams(dimension_semantics=("arbitrary",)),
        name="apply",
    )(high, low, flat)


def chunk_counts(states):
    rest = states - 1
    return [c for c in (1, rest // 2, rest - rest // 2) if c]


def per_device(devices, initial_states, potential, bounds):
    states, depth, rows, lanes = initial_states.shape
    points = depth * rows * lanes
    local = points // devices
    scal = filter_scalars(bounds)
    pieces = []
    begin = 0
    for count in chunk_counts(states):
        filtered = run_filter(scal, initial_states, potential, begin, count)
        if devices != depth:
            filtered = jnp.swapaxes(filtered, 0, 1).reshape(count, devices, local // lanes, lanes)
            filtered = jnp.swapaxes(filtered, 0, 1)
        pieces.append(lax.all_to_all(filtered, "state", split_axis=0, concat_axis=0, tiled=True))
        begin += count
    flat, gram = run_gram(pieces)
    total = gram.shape[0]
    blocks = gram.reshape(devices, total // devices, total)
    blocks = lax.all_to_all(blocks, "state", split_axis=0, concat_axis=0, tiled=True)
    mine = jnp.broadcast_to(jnp.sum(blocks, axis=0)[None], blocks.shape)
    gram = lax.all_to_all(mine, "state", split_axis=0, concat_axis=0, tiled=True)
    high, low = run_factor(gram.reshape(total, total), math.sqrt(points))
    return run_apply(high, low, flat)


def solution(mesh):
    return jax.shard_map(
        functools.partial(per_device, mesh.shape["state"]),
        mesh=mesh,
        in_specs=(P(("cuts", "state"), None, None, None), P(), P("cuts")),
        out_specs=P("cuts", "state"),
        check_vma=False,
    )
```

```python
import functools
import math

import jax
import jax.numpy as jnp
from jax import lax
from jax.experimental import pallas as pl
from jax.experimental.pallas import tpu as pltpu
from jax.sharding import PartitionSpec as P

DEGREE = 16
ANCHOR_VALUE = -1.125
SUB = 8
LANES = 128
BLOCK = 32


def filter_scalars(bounds, shape):
    low_end = jnp.full(shape, bounds[0], jnp.int32).astype(jnp.float32) / 64.0
    high_end = jnp.full(shape, bounds[1], jnp.int32).astype(jnp.float32) / 16.0
    half_width = (high_end - low_end) / 2.0
    centre = (high_end + low_end) / 2.0
    sigma_now = half_width / (ANCHOR_VALUE - centre)
    tau_value = 2.0 / sigma_now
    scale = sigma_now
    for _ in range(1, DEGREE):
        sigma_now = 1.0 / (tau_value - sigma_now)
        scale = scale * sigma_now
    return (-1.0 / 12.0) / half_width, 2.0 / half_width, 3.75 - centre, scale


def filter_kernel(bounds, states, potential, out, weight, first, second):
    depth, rows, lanes = out.shape
    tiles = rows // SUB
    line_w, twice, shift, scale = filter_scalars(bounds, (SUB, lanes))

    @pl.when(pl.program_id(0) == 0)
    def _():
        @pl.loop(0, depth, unroll=8)
        def _(z):
            for t in range(tiles):
                piece = potential[z, pl.ds(t, SUB, stride=tiles), :]
                weight[z, t] = (piece + shift) * twice

        for field in (first, second):
            for edge in (0, 1, depth + 2, depth + 3):
                field[edge] = jnp.zeros(field.shape[1:], jnp.float32)

    @pl.loop(0, depth, unroll=8)
    def _(z):
        out[z] = states[z].astype(jnp.float32)
        for t in range(tiles):
            first[z + 2, t] = out[z, pl.ds(t, SUB, stride=tiles), :]

    wrap = lax.broadcasted_iota(jnp.int32, (lanes, lanes), 0)
    wrap = jnp.abs(wrap - lax.broadcasted_iota(jnp.int32, (lanes, lanes), 1))
    wrap = jnp.minimum(wrap, lanes - wrap)
    ring = jnp.where(wrap == 1, 16.0, jnp.where(wrap == 2, -1.0, 0.0)).astype(jnp.bfloat16)
    ring = jnp.concatenate([ring, ring], axis=0)

    def applied(src):
        block = src[2 : depth + 2]
        along = block.reshape(depth * rows, lanes)
        along = dot(jnp.concatenate(split(along), axis=1), ring, ((1,), (0,)))
        along = along.reshape(block.shape)
        for z in range(depth):
            held = [block[z, t] for t in range(tiles)]
            back = {t: pltpu.roll(held[t], 1, 0) for t in (tiles - 1, tiles - 2)}
            ahead = {t: pltpu.roll(held[t], SUB - 1, 0) for t in (0, 1)}

            def at(t):
                if t < 0:
                    return back[t + tiles]
                if t >= tiles:
                    return ahead[t - tiles]
                return held[t]

            for t in range(tiles):
                near = (at(t - 1) + at(t + 1)) + (src[z + 1, t] + src[z + 3, t])
                far = (at(t - 2) + at(t + 2)) + (src[z, t] + src[z + 4, t])
                total = along[z, t] + (16.0 * near - far)
                yield z, t, total * line_w + held[t] * weight[z, t]

    def step(src, dst):
        for z, t, value in applied(src):
            dst[z + 2, t] = value - dst[z + 2, t]

    for z, t, value in applied(first):
        second[z + 2, t] = 0.5 * value

    @pl.loop(0, (DEGREE - 2) // 2)
    def _(_):
        step(second, first)
        step(first, second)

    for z, t, value in applied(second):
        out[z, pl.ds(t, SUB, stride=tiles), :] = (value - first[z + 2, t]) * scale


def run_filter(bounds, states, potential, begin, count):
    _, depth, rows, lanes = states.shape
    points = depth * rows * lanes
    field = pltpu.VMEM((depth + 4, rows // SUB, SUB, lanes), jnp.float32)
    return pl.pallas_call(
        filter_kernel,
        grid=(count,),
        in_specs=[
            pl.BlockSpec(memory_space=pltpu.SMEM),
            pl.BlockSpec((None, depth, rows, lanes), lambda i: (begin + i, 0, 0, 0)),
            pl.BlockSpec((depth, rows, lanes), lambda i: (0, 0, 0)),
        ],
        out_specs=pl.BlockSpec((depth, None, rows, lanes), lambda i: (0, i, 0, 0)),
        out_shape=jax.ShapeDtypeStruct((depth, count, rows, lanes), jnp.float32),
        scratch_shapes=[
            pltpu.VMEM((depth, rows // SUB, SUB, lanes), jnp.float32),
            field,
            field,
        ],
        compiler_params=pltpu.CompilerParams(dimension_semantics=("arbitrary",)),
        cost_estimate=pl.CostEstimate(
            flops=18 * DEGREE * points * count,
            bytes_accessed=points * (6 * count + 4),
            transcendentals=0,
        ),
        name=f"filter_{begin}",
    )(bounds, states, potential)


def split(value):
    high = value.astype(jnp.bfloat16)
    return high, (value - high.astype(jnp.float32)).astype(jnp.bfloat16)


def dot(left, right, dims):
    return lax.dot_general(left, right, (dims, ((), ())), preferred_element_type=jnp.float32)


def gather(pieces, tall, high, low):
    i = pl.program_id(0)
    begin = 0
    for piece in pieces:
        sources, count, _, lanes = piece.shape
        for j in range(count):
            where = slice(begin + j * sources, begin + (j + 1) * sources)
            value = jnp.swapaxes(piece[:, j, pl.ds(i * tall, tall), :], 0, 1)
            for r in range(tall):
                columns = slice(r * lanes, (r + 1) * lanes)
                high[where, columns], low[where, columns] = split(value[r])
        begin += count * sources


def accumulate(pairs):
    @pl.when(pl.program_id(0) == 0)
    def _():
        for ref, value in pairs:
            ref[...] = value

    @pl.when(pl.program_id(0) > 0)
    def _():
        for ref, value in pairs:
            ref[...] += value


def early_kernel(tall, *refs):
    *pieces, high, low, gram, same, cross = refs
    gather(pieces, tall, high, low)
    left = high[...]
    accumulate(
        [
            (same, dot(left, left, ((1,), (1,)))),
            (cross, dot(left, low[...], ((1,), (1,)))),
        ]
    )

    @pl.when(pl.program_id(0) == pl.num_programs(0) - 1)
    def _():
        gram[...] = same[...] + (cross[...] + cross[...].T)


def late_kernel(tall, early_high, early_low, early_gram, piece, *refs):
    high, low, gram, same, cross = refs
    gather([piece], tall, high, low)
    sources = piece.shape[0]
    old = early_high.shape[0]
    new = high.shape[0]
    left = high[...]
    both = jnp.concatenate([left, low[...]], axis=0)
    kept = jnp.concatenate([early_high[...], left], axis=0)
    accumulate(
        [
            (same, dot(both, kept, ((1,), (1,)))),
            (cross, dot(left, early_low[...], ((1,), (1,)))),
        ]
    )

    @pl.when(pl.program_id(0) == pl.num_programs(0) - 1)
    def _():
        total = old + new
        mixed = same[:new, :old] + (same[new:, :old] + cross[...])
        tail = same[new:, old:]
        own = same[:new, old:] + (tail + tail.T)
        top = jnp.concatenate([early_gram[...], mixed.T], axis=1)
        whole = jnp.concatenate([top, jnp.concatenate([mixed, own], axis=1)], axis=0)
        lines = gram.reshape(gram.shape[0] * gram.shape[1], LANES)
        per_device = total // sources
        for half in range(total // LANES):
            for c in range(per_device):
                where = pl.ds(half * per_device + c, sources, stride=gram.shape[1])
                block = whole[c * sources : (c + 1) * sources, half * LANES : (half + 1) * LANES]
                lines[where, :] = block


def run_gram(pieces):
    sources, _, rows, lanes = pieces[0].shape
    counts = [p.shape[1] for p in pieces]
    new = sources * counts[-1]
    old = sources * sum(counts[:-1])
    total = old + new
    tall = SUB if rows % SUB == 0 else rows
    points = rows * lanes
    resident = pl.BlockSpec(memory_space=pltpu.VMEM)

    def columns(count):
        return pl.BlockSpec((count, tall * lanes), lambda i: (0, i))

    def pair(count):
        return [jax.ShapeDtypeStruct((count, points), jnp.bfloat16)] * 2

    def fixed(*shape):
        return pl.BlockSpec(shape, lambda i: (0,) * len(shape))

    params = pltpu.CompilerParams(dimension_semantics=("arbitrary",))
    early_high, early_low, early_gram = pl.pallas_call(
        functools.partial(early_kernel, tall),
        grid=(rows // tall,),
        in_specs=[resident] * (len(pieces) - 1),
        out_specs=[columns(old), columns(old), fixed(old, old)],
        out_shape=[*pair(old), jax.ShapeDtypeStruct((old, old), jnp.float32)],
        scratch_shapes=[pltpu.VMEM((old, old), jnp.float32)] * 2,
        compiler_params=params,
        cost_estimate=pl.CostEstimate(
            flops=4 * old * old * points, bytes_accessed=8 * old * points, transcendentals=0
        ),
        name="early_gram",
    )(*pieces[:-1])
    blocks = (sources, total // LANES * (total // sources), LANES)
    high, low, gram = pl.pallas_call(
        functools.partial(late_kernel, tall),
        grid=(rows // tall,),
        in_specs=[columns(old), columns(old), fixed(old, old), resident],
        out_specs=[columns(new), columns(new), fixed(*blocks)],
        out_shape=[*pair(new), jax.ShapeDtypeStruct(blocks, jnp.float32)],
        scratch_shapes=[
            pltpu.VMEM((2 * new, total), jnp.float32),
            pltpu.VMEM((new, old), jnp.float32),
        ],
        compiler_params=params,
        name="late_gram",
    )(early_high, early_low, early_gram, pieces[-1])
    return (early_high, early_low, high, low), gram


def exact_dot(left, right, dims):
    return lax.dot_general(
        left,
        right,
        (dims, ((), ())),
        precision=lax.Precision.HIGHEST,
        preferred_element_type=jnp.float32,
    )


def eliminate(tiles):
    count = len(tiles)
    shape = tiles[0].shape
    line = lax.broadcasted_iota(jnp.int32, shape, 0)

    def row(tile, c):
        return jnp.broadcast_to(tile[c : c + 1, :], shape)

    cols = [
        {g: jnp.broadcast_to(tiles[g][:, d : d + 1], shape) for g in range(d // SUB, count)}
        for d in range(count * SUB)
    ]
    scales = [jnp.ones(shape, jnp.float32) for _ in range(count)]
    for j in range(0, count * SUB, 2):
        own, c = j // SUB, j % SUB
        left, right = cols[j], cols[j + 1]
        p, q, s = row(left[own], c), row(left[own], c + 1), row(right[own], c + 1)
        inverse = 1.0 / (p * s - q * q)
        p_in, q_in, s_in = p * inverse, q * inverse, s * inverse
        ratio = q / p
        row_left, row_right = row(tiles[own], c), row(tiles[own], c + 1)
        scales[own] = jnp.where(line == c, p, scales[own])
        scales[own] = jnp.where(line == c + 1, s - q * ratio, scales[own])
        first, second = {}, {}
        for g in range(own, count):
            first[g] = left[g] * s_in - right[g] * q_in
            second[g] = right[g] * p_in - left[g] * q_in
        first[own] = jnp.where(line > c + 1, first[own], jnp.where(line == c + 1, ratio, 0.0))
        second[own] = jnp.where(line > c + 1, second[own], 0.0)
        for d in range(j + 2, count * SUB):
            x, y = row(left[d // SUB], d % SUB), row(right[d // SUB], d % SUB)
            for g in range(d // SUB, count):
                cols[d][g] = cols[d][g] - (first[g] * x + second[g] * y)
        for g in range(own, count):
            tiles[g] = tiles[g] - (first[g] * row_left + second[g] * row_right)
    return [t * lax.rsqrt(v) for t, v in zip(tiles, scales)]


def finish_kernel(factor_scale, gram, *refs):
    rows, out, work, turn, right, stage, arrive, leave = refs[:4], *refs[4:]
    begin = (0, rows[0].shape[0])
    copies = [
        pltpu.make_async_copy(
            ref, right.at[i % 2, pl.ds(begin[i // 2], ref.shape[0])], arrive.at[i]
        )
        for i, ref in enumerate(rows)
    ]
    for copy in copies:
        copy.start()
    high, low = invert_factor(factor_scale, gram, work, turn)
    both = jnp.concatenate([high, low], axis=0)
    for copy in copies:
        copy.wait()
    size, wide = stage.shape[1:]
    sent = []
    for t in range(out.shape[1] // wide):
        columns = pl.ds(t * wide, wide)
        main = dot(both, right[0, :, columns], ((1,), (0,)))
        rest = dot(high, right[1, :, columns], ((1,), (0,)))
        if t >= 2:
            sent[t - 2].wait()
        stage[t % 2] = main[:size] + (main[size:] + rest)
        sent.append(pltpu.make_async_copy(stage.at[t % 2], out.at[:, columns], leave.at[t % 2]))
        sent[t].start()
    for copy in sent[-2:]:
        copy.wait()


def invert_factor(factor_scale, gram, work, turn):
    size = work.shape[0]
    sources, stride, _ = gram.shape
    halves = size // LANES
    per_device = size // sources
    lines = gram.reshape(sources * stride, LANES)
    for half in range(halves):
        for c in range(per_device):
            block = lines[pl.ds(half * per_device + c, sources, stride=stride), :]
            turn[half, pl.ds(c, sources, stride=per_device), :] = block
    whole = jnp.concatenate([turn[k] for k in range(halves)], axis=1).T
    to_states(whole, sources, turn)
    for k in range(halves):
        work[:, k * LANES : (k + 1) * LANES] = turn[k]
    rows = lax.broadcasted_iota(jnp.int32, (size, size), 0)
    cols = lax.broadcasted_iota(jnp.int32, (size, size), 1)
    work[:, size:] = jnp.where(rows == cols, 1.0, 0.0)
    lane = lax.broadcasted_iota(jnp.int32, (BLOCK, LANES), 1)
    line = lax.broadcasted_iota(jnp.int32, (BLOCK, LANES), 0)
    unit = jnp.where(lane == line + BLOCK, 1.0, 0.0)
    for k in range(0, size, BLOCK):
        diag = work[k : k + BLOCK, k : k + BLOCK]
        local = jnp.concatenate([diag, unit[:, BLOCK:]], axis=1)
        tiles = eliminate([local[i : i + SUB] for i in range(0, BLOCK, SUB)])
        inverse = jnp.concatenate(tiles, axis=0)[:, BLOCK : 2 * BLOCK]
        panel = exact_dot(inverse, work[k : k + BLOCK, :], ((1,), (0,)))
        work[k : k + BLOCK, :] = panel
        if k + BLOCK < size:
            below = panel[:, k + BLOCK : size]
            work[k + BLOCK :, :] -= exact_dot(below, panel, ((0,), (0,)))
    mixed = (work[:, size:] * factor_scale).T
    for k in range(halves):
        turn[k] = mixed[:, k * LANES : (k + 1) * LANES]
    columns = [
        jnp.concatenate(
            [turn[k, pl.ds(c, sources, stride=per_device), :] for c in range(per_device)], axis=0
        )
        for k in range(halves)
    ]
    return split(jnp.concatenate(columns, axis=1).T)


def to_states(whole, sources, turn):
    size = whole.shape[0]
    per_device = size // sources
    for c in range(per_device):
        for k in range(size // LANES):
            block = whole[c * sources : (c + 1) * sources, k * LANES : (k + 1) * LANES]
            turn[k, pl.ds(c, sources, stride=per_device), :] = block


def run_finish(gram, rows, factor_scale):
    sources, stride, lanes = gram.shape
    size = math.isqrt(sources * stride * lanes)
    points = rows[0].shape[1]
    wide = 1024 if points % 1024 == 0 else 512
    anywhere = pl.BlockSpec(memory_space=pl.ANY)
    return pl.pallas_call(
        functools.partial(finish_kernel, factor_scale),
        in_specs=[pl.BlockSpec(memory_space=pltpu.VMEM)] + [anywhere] * len(rows),
        out_specs=anywhere,
        out_shape=jax.ShapeDtypeStruct((size, points), jnp.float32),
        scratch_shapes=[
            pltpu.VMEM((size, 2 * size), jnp.float32),
            pltpu.VMEM((size // LANES, size, LANES), jnp.float32),
            pltpu.VMEM((2, size, points), jnp.bfloat16),
            pltpu.VMEM((2, size, wide), jnp.float32),
            pltpu.SemaphoreType.DMA((len(rows),)),
            pltpu.SemaphoreType.DMA((2,)),
        ],
        name="finish",
    )(gram, *rows)


def chunk_counts(states):
    edge = max(states // 4, 1)
    return [c for c in (edge, states - 2 * edge, edge) if c > 0]


def per_device(devices, initial_states, potential, bounds):
    states, depth, rows, lanes = initial_states.shape
    points = depth * rows * lanes
    local = points // devices
    pieces = []
    begin = 0
    for count in chunk_counts(states):
        filtered = run_filter(bounds, initial_states, potential, begin, count)
        if devices != depth:
            filtered = jnp.swapaxes(filtered, 0, 1).reshape(count, devices, local // lanes, lanes)
            filtered = jnp.swapaxes(filtered, 0, 1)
        pieces.append(lax.all_to_all(filtered, "state", split_axis=0, concat_axis=0, tiled=True))
        begin += count
    rows, gram = run_gram(pieces)
    gram = lax.all_to_all(gram, "state", split_axis=0, concat_axis=0, tiled=True)
    gram = jnp.broadcast_to(jnp.sum(gram, axis=0)[None], gram.shape)
    gram = lax.all_to_all(gram, "state", split_axis=0, concat_axis=0, tiled=True)
    return run_finish(gram, rows, math.sqrt(points))


def solution(mesh):
    return jax.shard_map(
        functools.partial(per_device, mesh.shape["state"]),
        mesh=mesh,
        in_specs=(P(("cuts", "state"), None, None, None), P(), P("cuts")),
        out_specs=P("cuts", "state"),
        check_vma=False,
    )
```

```python
import functools
import math

import jax
import jax.numpy as jnp
from jax import lax
from jax.experimental import pallas as pl
from jax.experimental.pallas import tpu as pltpu
from jax.sharding import PartitionSpec as P

DEGREE = 16
ANCHOR_VALUE = -1.125
SUB = 8
LANES = 128
BLOCK = 32


def filter_scalars(bounds, shape):
    low_end = jnp.full(shape, bounds[0], jnp.int32).astype(jnp.float32) / 64.0
    high_end = jnp.full(shape, bounds[1], jnp.int32).astype(jnp.float32) / 16.0
    half_width = (high_end - low_end) / 2.0
    centre = (high_end + low_end) / 2.0
    sigma_now = half_width / (ANCHOR_VALUE - centre)
    tau_value = 2.0 / sigma_now
    scale = sigma_now
    for _ in range(1, DEGREE):
        sigma_now = 1.0 / (tau_value - sigma_now)
        scale = scale * sigma_now
    return (-1.0 / 12.0) / half_width, 2.0 / half_width, 3.75 - centre, scale


def filter_kernel(bounds, states, potential, out, weight, first, second):
    depth, rows, lanes = out.shape
    tiles = rows // SUB
    line_w, twice, shift, scale = filter_scalars(bounds, (SUB, lanes))

    @pl.when(pl.program_id(0) == 0)
    def _():
        @pl.loop(0, depth, unroll=8)
        def _(z):
            for t in range(tiles):
                piece = potential[z, pl.ds(t, SUB, stride=tiles), :]
                weight[z, t] = (piece + shift) * twice

        for field in (first, second):
            for edge in (0, 1, depth + 2, depth + 3):
                field[edge] = jnp.zeros(field.shape[1:], jnp.float32)

    @pl.loop(0, depth, unroll=8)
    def _(z):
        out[z] = states[z].astype(jnp.float32)
        for t in range(tiles):
            first[z + 2, t] = out[z, pl.ds(t, SUB, stride=tiles), :]

    wrap = lax.broadcasted_iota(jnp.int32, (lanes, lanes), 0)
    wrap = jnp.abs(wrap - lax.broadcasted_iota(jnp.int32, (lanes, lanes), 1))
    wrap = jnp.minimum(wrap, lanes - wrap)
    ring = jnp.where(wrap == 1, 16.0, jnp.where(wrap == 2, -1.0, 0.0)).astype(jnp.bfloat16)
    ring = jnp.concatenate([ring, ring], axis=0)

    def applied(src):
        block = src[2 : depth + 2]
        along = block.reshape(depth * rows, lanes)
        along = dot(jnp.concatenate(split(along), axis=1), ring, ((1,), (0,)))
        along = along.reshape(block.shape)
        for z in range(depth):
            held = [block[z, t] for t in range(tiles)]
            back = {t: pltpu.roll(held[t], 1, 0) for t in (tiles - 1, tiles - 2)}
            ahead = {t: pltpu.roll(held[t], SUB - 1, 0) for t in (0, 1)}

            def at(t):
                if t < 0:
                    return back[t + tiles]
                if t >= tiles:
                    return ahead[t - tiles]
                return held[t]

            for t in range(tiles):
                near = (at(t - 1) + at(t + 1)) + (src[z + 1, t] + src[z + 3, t])
                far = (at(t - 2) + at(t + 2)) + (src[z, t] + src[z + 4, t])
                total = along[z, t] + (16.0 * near - far)
                yield z, t, total * line_w + held[t] * weight[z, t]

    def step(src, dst):
        for z, t, value in applied(src):
            dst[z + 2, t] = value - dst[z + 2, t]

    for z, t, value in applied(first):
        second[z + 2, t] = 0.5 * value

    @pl.loop(0, (DEGREE - 2) // 2)
    def _(_):
        step(second, first)
        step(first, second)

    for z, t, value in applied(second):
        out[z, pl.ds(t, SUB, stride=tiles), :] = (value - first[z + 2, t]) * scale


def run_filter(bounds, states, potential, begin, count):
    _, depth, rows, lanes = states.shape
    points = depth * rows * lanes
    field = pltpu.VMEM((depth + 4, rows // SUB, SUB, lanes), jnp.float32)
    return pl.pallas_call(
        filter_kernel,
        grid=(count,),
        in_specs=[
            pl.BlockSpec(memory_space=pltpu.SMEM),
            pl.BlockSpec((None, depth, rows, lanes), lambda i: (begin + i, 0, 0, 0)),
            pl.BlockSpec((depth, rows, lanes), lambda i: (0, 0, 0)),
        ],
        out_specs=pl.BlockSpec((depth, None, rows, lanes), lambda i: (0, i, 0, 0)),
        out_shape=jax.ShapeDtypeStruct((depth, count, rows, lanes), jnp.float32),
        scratch_shapes=[
            pltpu.VMEM((depth, rows // SUB, SUB, lanes), jnp.float32),
            field,
            field,
        ],
        compiler_params=pltpu.CompilerParams(dimension_semantics=("arbitrary",)),
        cost_estimate=pl.CostEstimate(
            flops=18 * DEGREE * points * count,
            bytes_accessed=points * (6 * count + 4),
            transcendentals=0,
        ),
        name=f"filter_{begin}",
    )(bounds, states, potential)


def split(value):
    high = value.astype(jnp.bfloat16)
    return high, (value - high.astype(jnp.float32)).astype(jnp.bfloat16)


def dot(left, right, dims):
    return lax.dot_general(left, right, (dims, ((), ())), preferred_element_type=jnp.float32)


def gather(pieces, tall, high, low):
    i = pl.program_id(0)
    begin = 0
    for piece in pieces:
        sources, count, _, lanes = piece.shape
        for j in range(count):
            where = slice(begin + j * sources, begin + (j + 1) * sources)
            value = jnp.swapaxes(piece[:, j, pl.ds(i * tall, tall), :], 0, 1)
            for r in range(tall):
                columns = slice(r * lanes, (r + 1) * lanes)
                high[where, columns], low[where, columns] = split(value[r])
        begin += count * sources


def accumulate(pairs):
    @pl.when(pl.program_id(0) == 0)
    def _():
        for ref, value in pairs:
            ref[...] = value

    @pl.when(pl.program_id(0) > 0)
    def _():
        for ref, value in pairs:
            ref[...] += value


def early_kernel(tall, *refs):
    *pieces, high, low, gram, same, cross = refs
    gather(pieces, tall, high, low)
    left = high[...]
    accumulate(
        [
            (same, dot(left, left, ((1,), (1,)))),
            (cross, dot(left, low[...], ((1,), (1,)))),
        ]
    )

    @pl.when(pl.program_id(0) == pl.num_programs(0) - 1)
    def _():
        gram[...] = same[...] + (cross[...] + cross[...].T)


def late_kernel(tall, early_high, early_low, early_gram, piece, *refs):
    high, low, gram, same, cross = refs
    gather([piece], tall, high, low)
    sources = piece.shape[0]
    old = early_high.shape[0]
    new = high.shape[0]
    left = high[...]
    both = jnp.concatenate([left, low[...]], axis=0)
    kept = jnp.concatenate([early_high[...], left], axis=0)
    accumulate(
        [
            (same, dot(both, kept, ((1,), (1,)))),
            (cross, dot(left, early_low[...], ((1,), (1,)))),
        ]
    )

    @pl.when(pl.program_id(0) == pl.num_programs(0) - 1)
    def _():
        total = old + new
        mixed = same[:new, :old] + (same[new:, :old] + cross[...])
        tail = same[new:, old:]
        own = same[:new, old:] + (tail + tail.T)
        top = jnp.concatenate([early_gram[...], mixed.T], axis=1)
        whole = jnp.concatenate([top, jnp.concatenate([mixed, own], axis=1)], axis=0)
        lines = gram.reshape(gram.shape[0] * gram.shape[1], LANES)
        per_device = total // sources
        for half in range(total // LANES):
            for c in range(per_device):
                where = pl.ds(half * per_device + c, sources, stride=gram.shape[1])
                block = whole[c * sources : (c + 1) * sources, half * LANES : (half + 1) * LANES]
                lines[where, :] = block


def run_gram(pieces):
    sources, _, rows, lanes = pieces[0].shape
    counts = [p.shape[1] for p in pieces]
    new = sources * counts[-1]
    old = sources * sum(counts[:-1])
    total = old + new
    tall = SUB if rows % SUB == 0 else rows
    points = rows * lanes
    resident = pl.BlockSpec(memory_space=pltpu.VMEM)

    def columns(count):
        return pl.BlockSpec((count, tall * lanes), lambda i: (0, i))

    def pair(count):
        return [jax.ShapeDtypeStruct((count, points), jnp.bfloat16)] * 2

    def fixed(*shape):
        return pl.BlockSpec(shape, lambda i: (0,) * len(shape))

    params = pltpu.CompilerParams(dimension_semantics=("arbitrary",))
    early_high, early_low, early_gram = pl.pallas_call(
        functools.partial(early_kernel, tall),
        grid=(rows // tall,),
        in_specs=[resident] * (len(pieces) - 1),
        out_specs=[columns(old), columns(old), fixed(old, old)],
        out_shape=[*pair(old), jax.ShapeDtypeStruct((old, old), jnp.float32)],
        scratch_shapes=[pltpu.VMEM((old, old), jnp.float32)] * 2,
        compiler_params=params,
        cost_estimate=pl.CostEstimate(
            flops=4 * old * old * points, bytes_accessed=8 * old * points, transcendentals=0
        ),
        name="early_gram",
    )(*pieces[:-1])
    blocks = (sources, total // LANES * (total // sources), LANES)
    high, low, gram = pl.pallas_call(
        functools.partial(late_kernel, tall),
        grid=(rows // tall,),
        in_specs=[columns(old), columns(old), fixed(old, old), resident],
        out_specs=[columns(new), columns(new), fixed(*blocks)],
        out_shape=[*pair(new), jax.ShapeDtypeStruct(blocks, jnp.float32)],
        scratch_shapes=[
            pltpu.VMEM((2 * new, total), jnp.float32),
            pltpu.VMEM((new, old), jnp.float32),
        ],
        compiler_params=params,
        name="late_gram",
    )(early_high, early_low, early_gram, pieces[-1])
    return (early_high, early_low, high, low), gram


def exact_dot(left, right, dims):
    return lax.dot_general(
        left,
        right,
        (dims, ((), ())),
        precision=lax.Precision.HIGHEST,
        preferred_element_type=jnp.float32,
    )


def eliminate(tiles):
    count = len(tiles)
    shape = tiles[0].shape
    line = lax.broadcasted_iota(jnp.int32, shape, 0)

    def row(tile, c):
        return jnp.broadcast_to(tile[c : c + 1, :], shape)

    cols = [
        {g: jnp.broadcast_to(tiles[g][:, d : d + 1], shape) for g in range(d // SUB, count)}
        for d in range(count * SUB)
    ]
    scales = [jnp.ones(shape, jnp.float32) for _ in range(count)]
    for j in range(0, count * SUB, 2):
        own, c = j // SUB, j % SUB
        left, right = cols[j], cols[j + 1]
        p, q, s = row(left[own], c), row(left[own], c + 1), row(right[own], c + 1)
        inverse = 1.0 / (p * s - q * q)
        p_in, q_in, s_in = p * inverse, q * inverse, s * inverse
        ratio = q / p
        row_left, row_right = row(tiles[own], c), row(tiles[own], c + 1)
        scales[own] = jnp.where(line == c, p, scales[own])
        scales[own] = jnp.where(line == c + 1, s - q * ratio, scales[own])
        first, second = {}, {}
        for g in range(own, count):
            first[g] = left[g] * s_in - right[g] * q_in
            second[g] = right[g] * p_in - left[g] * q_in
        first[own] = jnp.where(line > c + 1, first[own], jnp.where(line == c + 1, ratio, 0.0))
        second[own] = jnp.where(line > c + 1, second[own], 0.0)
        for d in range(j + 2, count * SUB):
            x, y = row(left[d // SUB], d % SUB), row(right[d // SUB], d % SUB)
            for g in range(d // SUB, count):
                cols[d][g] = cols[d][g] - (first[g] * x + second[g] * y)
        for g in range(own, count):
            tiles[g] = tiles[g] - (first[g] * row_left + second[g] * row_right)
    return [t * lax.rsqrt(v) for t, v in zip(tiles, scales)]


def finish_kernel(factor_scale, gram, *refs):
    rows, out, work, turn, right, stage, arrive, leave = refs[:4], *refs[4:]
    begin = (0, rows[0].shape[0])
    copies = [
        pltpu.make_async_copy(
            ref, right.at[i % 2, pl.ds(begin[i // 2], ref.shape[0])], arrive.at[i]
        )
        for i, ref in enumerate(rows)
    ]
    for copy in copies:
        copy.start()
    slots, height, wide = stage.shape
    sent = []
    for half, (high, low) in enumerate(invert_factor(factor_scale, gram, work, turn)):
        if half == 0:
            for copy in copies:
                copy.wait()
        both = jnp.concatenate([high, low], axis=0)
        lines = pl.ds(half * height, height)
        for t in range(out.shape[1] // wide):
            columns = pl.ds(t * wide, wide)
            main = dot(both, right[0, :, columns], ((1,), (0,)))
            rest = dot(high, right[1, :, columns], ((1,), (0,)))
            slot = len(sent) % slots
            if len(sent) >= slots:
                sent[len(sent) - slots].wait()
            stage[slot] = main[:height] + (main[height:] + rest)
            sent.append(
                pltpu.make_async_copy(stage.at[slot], out.at[lines, columns], leave.at[slot])
            )
            sent[-1].start()
    for copy in sent[-slots:]:
        copy.wait()


def invert_factor(factor_scale, gram, work, turn):
    size = work.shape[0]
    sources, stride, _ = gram.shape
    halves = size // LANES
    per_device = size // sources
    lines = gram.reshape(sources * stride, LANES)
    for half in range(halves):
        for c in range(per_device):
            block = lines[pl.ds(half * per_device + c, sources, stride=stride), :]
            turn[half, pl.ds(c, sources, stride=per_device), :] = block
    whole = jnp.concatenate([turn[k] for k in range(halves)], axis=1).T
    to_states(whole, sources, turn)
    for k in range(halves):
        work[:, k * LANES : (k + 1) * LANES] = turn[k]
    rows = lax.broadcasted_iota(jnp.int32, (size, size), 0)
    cols = lax.broadcasted_iota(jnp.int32, (size, size), 1)
    work[:, size:] = jnp.where(rows == cols, 1.0, 0.0)
    lane = lax.broadcasted_iota(jnp.int32, (BLOCK, LANES), 1)
    line = lax.broadcasted_iota(jnp.int32, (BLOCK, LANES), 0)
    unit = jnp.where(lane == line + BLOCK, 1.0, 0.0)
    for k in range(0, size, BLOCK):
        diag = work[k : k + BLOCK, k : k + BLOCK]
        local = jnp.concatenate([diag, unit[:, BLOCK:]], axis=1)
        tiles = eliminate([local[i : i + SUB] for i in range(0, BLOCK, SUB)])
        inverse = jnp.concatenate(tiles, axis=0)[:, BLOCK : 2 * BLOCK]
        panel = exact_dot(inverse, work[k : k + BLOCK, :], ((1,), (0,)))
        work[k : k + BLOCK, :] = panel
        if k + BLOCK < size:
            below = panel[:, k + BLOCK : size]
            work[k + BLOCK :, :] -= exact_dot(below, panel, ((0,), (0,)))
        if (k + BLOCK) % LANES == 0:
            half = k // LANES
            final = work[half * LANES : (half + 1) * LANES, size:] * factor_scale
            turn[half] = final.T
            parts = [
                turn[half, pl.ds(c, sources, stride=per_device), :] for c in range(per_device)
            ]
            yield split(jnp.concatenate(parts, axis=0).T)


def to_states(whole, sources, turn):
    size = whole.shape[0]
    per_device = size // sources
    for c in range(per_device):
        for k in range(size // LANES):
            block = whole[c * sources : (c + 1) * sources, k * LANES : (k + 1) * LANES]
            turn[k, pl.ds(c, sources, stride=per_device), :] = block


def run_finish(gram, rows, factor_scale):
    sources, stride, lanes = gram.shape
    size = math.isqrt(sources * stride * lanes)
    points = rows[0].shape[1]
    wide = 1024 if points % 1024 == 0 else 512
    anywhere = pl.BlockSpec(memory_space=pl.ANY)
    return pl.pallas_call(
        functools.partial(finish_kernel, factor_scale),
        in_specs=[pl.BlockSpec(memory_space=pltpu.VMEM)] + [anywhere] * len(rows),
        out_specs=anywhere,
        out_shape=jax.ShapeDtypeStruct((size, points), jnp.float32),
        scratch_shapes=[
            pltpu.VMEM((size, 2 * size), jnp.float32),
            pltpu.VMEM((size // LANES, size, LANES), jnp.float32),
            pltpu.VMEM((2, size, points), jnp.bfloat16),
            pltpu.VMEM((points // wide, LANES, wide), jnp.float32),
            pltpu.SemaphoreType.DMA((len(rows),)),
            pltpu.SemaphoreType.DMA((points // wide,)),
        ],
        name="finish",
    )(gram, *rows)


def chunk_counts(states):
    edge = max(states // 4, 1)
    return [c for c in (edge, states - 2 * edge, edge) if c > 0]


def per_device(devices, initial_states, potential, bounds):
    states, depth, rows, lanes = initial_states.shape
    points = depth * rows * lanes
    local = points // devices
    pieces = []
    begin = 0
    for count in chunk_counts(states):
        filtered = run_filter(bounds, initial_states, potential, begin, count)
        if devices != depth:
            filtered = jnp.swapaxes(filtered, 0, 1).reshape(count, devices, local // lanes, lanes)
            filtered = jnp.swapaxes(filtered, 0, 1)
        pieces.append(lax.all_to_all(filtered, "state", split_axis=0, concat_axis=0, tiled=True))
        begin += count
    rows, gram = run_gram(pieces)
    gram = lax.all_to_all(gram, "state", split_axis=0, concat_axis=0, tiled=True)
    gram = jnp.broadcast_to(jnp.sum(gram, axis=0)[None], gram.shape)
    gram = lax.all_to_all(gram, "state", split_axis=0, concat_axis=0, tiled=True)
    return run_finish(gram, rows, math.sqrt(points))


def solution(mesh):
    return jax.shard_map(
        functools.partial(per_device, mesh.shape["state"]),
        mesh=mesh,
        in_specs=(P(("cuts", "state"), None, None, None), P(), P("cuts")),
        out_specs=P("cuts", "state"),
        check_vma=False,
    )
```
